32 devices in a mesh: img: 4 (over y, x), rows: 8 (over z, core).
Axes of the slice: x: 2, y: 2, z: 4, core: 2. Of those that a mesh axis runs over, the one named last changes fastest.
Arguments:
- features: bfloat16 [8, 16, 256, 512], P('img', 'rows'), parts along dimension 0, may hold values from -100 to 100
- conv_first: bfloat16 [3, 3, 512, 512], replicated, may hold values from -0.09375 to 0.09375
- conv_second: bfloat16 [3, 3, 512, 512], replicated, may hold values from -0.09375 to 0.09375
- query_weight: bfloat16 [512, 512], replicated, may hold values from -0.25 to 0.25
- key_weight: bfloat16 [512, 512], replicated, may hold values from -0.25 to 0.25
- value_weight: bfloat16 [512, 512], replicated, may hold values from -0.25 to 0.25
- output_weight: bfloat16 [512, 512], replicated, may hold values from -0.25 to 0.25
- time_weight: bfloat16 [256, 1024], replicated, may hold values from -0.375 to 0.375
- norm_gains: float32 [3, 512], replicated, may hold values from 0.1 to 1.9
- norm_shifts: float32 [3, 512], replicated, may hold values from -3 to 3
- text_states: bfloat16 [8, 128, 512], P('img'), parts along dimension 0, may hold values from -500 to 500
- timestep: int32 [8], P('img'), parts along dimension 0, may hold values from 0 to 999
- aug_level: int32 [8], P('img'), parts along dimension 0, may hold values from 0 to 999
- text_length: int32 [8], P('img'), parts along dimension 0, may hold values from 2 to 128
Outputs:
- block_output: bfloat16 [8, 16, 256, 512], P('img', 'rows'), parts along dimension 0
The draws below stay inside these ranges and needn't reach their ends.
There are 4 independent parts, one for each index of `img`. The reference program is written for one: setup_inputs(seed, part) draws one part's arguments, and reference() takes and returns one part's arrays. A program takes and returns all parts, laid end to end along the dimension named above; an argument that names none is the same for every part. Nothing has to cross between parts.
All inputs are finite; a program needn't handle non-finite values.
Results may differ from the reference program's by a relative error of at most 0.035.
Values may be sent and summed in bfloat16 or wider, within the bound.
A program may use at most 128 MiB of HBM per device.

```python
import math
import jax
import jax.numpy as jnp
from jax import lax

C = 512
GROUPS = 32
HEADS = 8
HEAD_DIM = 64
TFREQ = 64
TXT = 128
IMAGES = 2
COLS = 256
H = 16


def draw_features(key, part):
    keys_all = jax.random.split(key, 7)
    full_shape = (IMAGES, H, COLS, C)
    base_draw = jax.random.truncated_normal(keys_all[0], -6.0, 6.0, full_shape, jnp.float32)
    trend = math.log(3.0)
    row_spread = 1.2
    raw_field = jax.random.truncated_normal(keys_all[5], -5.0, 5.0, (IMAGES, H, COLS + 4), jnp.float32)
    smooth_field = raw_field[:, :, 0:COLS] + raw_field[:, :, 1:COLS + 1] + raw_field[:, :, 2:COLS + 2] + raw_field[:, :, 3:COLS + 3] + raw_field[:, :, 4:COLS + 4]
    smooth_field = smooth_field / math.sqrt(5.0)
    sign_pattern = jnp.where(jax.random.bernoulli(keys_all[6], 0.5, (C,)), 1.0, -1.0).astype(jnp.float32)
    shared_part = smooth_field[:, :, :, None] * sign_pattern[None, None, None, :]
    mixed_draw = 0.4 * base_draw + 0.9 * shared_part
    row_ramp = jnp.arange(H, dtype=jnp.float32) / (H - 1)
    row_scale = jnp.exp(trend * (row_ramp - 0.5)[None, :] + jax.random.uniform(keys_all[1], (IMAGES, H), jnp.float32, -row_spread, row_spread))
    row_offset = 0.8 * jax.random.truncated_normal(keys_all[4], -3.0, 3.0, (IMAGES, H), jnp.float32)
    col_scale = jnp.exp(jax.random.uniform(keys_all[2], (COLS,), jnp.float32, -0.4, 0.4))
    chan_scale = jnp.exp(jax.random.uniform(keys_all[3], (C,), jnp.float32, -0.35, 0.35))
    scaled = 0.6 * mixed_draw * row_scale[:, :, None, None] * col_scale[None, None, :, None] * chan_scale + row_offset[:, :, None, None]
    return jnp.clip(scaled, -100.0, 100.0).astype(jnp.bfloat16)


def draw_text_states(key, part):
    keys_all = jax.random.split(key, 1)
    full_shape = (IMAGES, TXT, C)
    base_draw = jax.random.truncated_normal(keys_all[0], -5.0, 5.0, full_shape, jnp.float32)
    return base_draw.astype(jnp.bfloat16)


def bell_draw(rng, dims, width, limit, held_as=jnp.bfloat16):
    entries = width * jax.random.normal(rng, dims, jnp.float32)
    return jnp.clip(entries, min=-limit, max=limit).astype(held_as)


def setup_inputs(seed: int = 0, part: int = 0) -> dict:
    key_list = jax.random.split(jax.random.key(seed), 15)
    part_splits = jax.random.split(jax.random.fold_in(key_list[14], part), 15)
    features = draw_features(jax.random.fold_in(jax.random.fold_in(key_list[14], part), 71), part)
    conv_first = bell_draw(key_list[1], (3, 3, C, C), (9 * C) ** -0.5, 0.09375)
    conv_second = bell_draw(key_list[2], (3, 3, C, C), (9 * C) ** -0.5, 0.09375)
    query_weight = bell_draw(key_list[3], (C, C), C ** -0.5, 0.25)
    key_weight = bell_draw(key_list[4], (C, C), C ** -0.5, 0.25)
    value_weight = bell_draw(key_list[5], (C, C), C ** -0.5, 0.25)
    output_weight = bell_draw(key_list[6], (C, C), C ** -0.5, 0.25)
    time_weight = bell_draw(key_list[7], (4 * TFREQ, 2 * C), (4 * TFREQ) ** -0.5, 0.375)
    norm_gains = jnp.clip(1.0 + 0.18 * jax.random.normal(key_list[8], (3, C), jnp.float32), 0.1, 1.9)
    norm_shifts = bell_draw(key_list[9], (3, C), 0.5, 3.0, jnp.float32)
    text_states = draw_text_states(jax.random.fold_in(jax.random.fold_in(key_list[14], part), 71), part)
    timestep = jax.random.randint(part_splits[11], (IMAGES,), 0, 1000).astype(jnp.int32)
    aug_level = jax.random.randint(part_splits[12], (IMAGES,), 0, 1000).astype(jnp.int32)
    text_length = jax.random.randint(part_splits[13], (IMAGES,), 2, TXT + 1).astype(jnp.int32)
    return {"features": features, "conv_first": conv_first, "conv_second": conv_second, "query_weight": query_weight, "key_weight": key_weight, "value_weight": value_weight, "output_weight": output_weight, "time_weight": time_weight, "norm_gains": norm_gains, "norm_shifts": norm_shifts, "text_states": text_states, "timestep": timestep, "aug_level": aug_level, "text_length": text_length}


EPSILON = 1e-05

def to_groups(per_channel):
    return per_channel.reshape(per_channel.shape[0], GROUPS, -1).sum(axis=2)

def to_channels(per_group, channels):
    return jnp.repeat(per_group, channels // GROUPS, axis=1)[:, None, None, :]

def normalize(values):
    channels = values.shape[3]
    cells_count = values.shape[1] * values.shape[2] * (channels // GROUPS)
    group_mean = to_groups(values.sum(axis=(1, 2))) / cells_count
    centered = values - to_channels(group_mean, channels)
    spread = to_groups(jnp.square(centered).sum(axis=(1, 2))) / cells_count
    return centered * to_channels(lax.rsqrt(spread + EPSILON), channels)

def sinusoid(steps):
    freqs = jnp.exp(jnp.arange(TFREQ, dtype=jnp.float32) * (-math.log(10000.0) / TFREQ))
    angles = steps.astype(jnp.float32)[:, None] * freqs[None, :]
    return jnp.concatenate([jnp.sin(angles), jnp.cos(angles)], axis=1)

def conditioning(timestep, aug_level, time_weight, channels):
    embedded = jnp.concatenate([sinusoid(timestep), sinusoid(aug_level)], axis=1).astype(jnp.bfloat16)
    film_terms = jnp.dot(embedded, time_weight, preferred_element_type=jnp.float32)
    return (film_terms[:, None, None, :channels], film_terms[:, None, None, channels:])

def convolve(padded_rows, weight):
    images, rows_in, col_count, channels = padded_rows.shape
    out_rows = rows_in - 2
    padded = jnp.pad(padded_rows, ((0, 0), (0, 0), (1, 1), (0, 0)))
    widened = jnp.concatenate([padded[:, :, 0:col_count], padded[:, :, 1:col_count + 1], padded[:, :, 2:col_count + 2]], axis=3)
    stacked = weight.reshape(3, 3 * channels, channels)
    total = jnp.zeros((images * out_rows * col_count, channels), jnp.float32)
    for offset in range(3):
        window = widened[:, offset:offset + out_rows].reshape(-1, 3 * channels)
        total = total + jnp.dot(window, stacked[offset], preferred_element_type=jnp.float32)
    return total.reshape(images, out_rows, col_count, channels)

def cross_attend(normed, text_states, text_length, query_weight, key_weight, value_weight, output_weight):
    images, rows_here, col_count, channels = normed.shape
    queries = jnp.dot(normed.reshape(-1, channels), query_weight, preferred_element_type=jnp.float32).astype(jnp.bfloat16)
    queries = queries.reshape(images, rows_here * col_count, HEADS, HEAD_DIM)
    flat_text = text_states.reshape(-1, channels)
    key_rows = jnp.dot(flat_text, key_weight, preferred_element_type=jnp.float32).astype(jnp.bfloat16)
    key_rows = key_rows.reshape(images, TXT, HEADS, HEAD_DIM)
    value_rows = jnp.dot(flat_text, value_weight, preferred_element_type=jnp.float32).astype(jnp.bfloat16)
    value_rows = value_rows.reshape(images, TXT, HEADS, HEAD_DIM)
    scores = jnp.einsum('iqhd,ikhd->ihqk', queries.astype(jnp.float32), key_rows.astype(jnp.float32)) * HEAD_DIM ** (-0.5)
    inside = (jnp.arange(TXT)[None, :] < text_length[:, None])[:, None, None, :]
    scores = jnp.where(inside, scores, -jnp.inf)
    highest = lax.optimization_barrier(jnp.max(scores, axis=3, keepdims=True))
    raised = jnp.exp(scores - highest)
    attention = (raised / lax.optimization_barrier(jnp.sum(raised, axis=3, keepdims=True))).astype(jnp.bfloat16)
    mixed_heads = jnp.einsum('ihqk,ikhd->iqhd', attention.astype(jnp.float32), value_rows.astype(jnp.float32)).astype(jnp.bfloat16)
    projected = jnp.dot(mixed_heads.reshape(-1, channels), output_weight, preferred_element_type=jnp.float32)
    return projected.reshape(images, rows_here, col_count, channels)

def reference(features, conv_first, conv_second, query_weight, key_weight, value_weight, output_weight, time_weight, norm_gains, norm_shifts, text_states, timestep, aug_level, text_length):
    channels = features.shape[3]
    residual = features.astype(jnp.float32)
    row_pad = ((0, 0), (1, 1), (0, 0), (0, 0))
    first_act = jax.nn.silu(normalize(residual) * norm_gains[0] + norm_shifts[0]).astype(jnp.bfloat16)
    hidden_one = convolve(jnp.pad(first_act, row_pad), conv_first)
    film_scale, film_shift = conditioning(timestep, aug_level, time_weight, channels)
    second_act = jax.nn.silu((normalize(hidden_one) * norm_gains[1] + norm_shifts[1]) * (1.0 + film_scale) + film_shift).astype(jnp.bfloat16)
    block_out = (residual + convolve(jnp.pad(second_act, row_pad), conv_second)).astype(jnp.bfloat16)
    normed = (normalize(block_out.astype(jnp.float32)) * norm_gains[2] + norm_shifts[2]).astype(jnp.bfloat16)
    attended = cross_attend(normed, text_states, text_length, query_weight, key_weight, value_weight, output_weight)
    return (block_out.astype(jnp.float32) + attended).astype(jnp.bfloat16)
```

```python
import functools
import math

import jax
import jax.numpy as jnp
from jax import lax
from jax.experimental import pallas as pl
from jax.experimental.pallas import tpu as pltpu
from jax.sharding import PartitionSpec as P

GROUPS = 32
HEADS = 8
HEAD_DIM = 64
TFREQ = 64
EPSILON = 1e-05
LANES = 128
CHUNK = 64
F32 = jnp.float32
BF16 = jnp.bfloat16
MESH = pl.DeviceIdType.MESH


def sine(angle):
    turns = jnp.floor(angle * (0.5 / math.pi) + 0.5)
    x = (angle - turns * 6.28125) - turns * (2.0 * math.pi - 6.28125)
    square = x * x
    total = jnp.full_like(x, 1.0 / math.factorial(17))
    for power in (15, 13, 11, 9, 7, 5, 3, 1):
        sign = -1.0 if (power // 2) % 2 else 1.0
        total = total * square + sign / math.factorial(power)
    return total * x


def group_totals(tile, size):
    lane = lax.broadcasted_iota(jnp.int32, tile.shape, 1)
    step = 1
    while step < size:
        up = pltpu.roll(tile, LANES - step, axis=1)
        down = pltpu.roll(tile, step, axis=1)
        tile = tile + jnp.where(lane % (2 * step) < step, up, down)
        step *= 2
    return tile


def wide(tile):
    return jnp.concatenate([tile[i : i + 1] for i in range(tile.shape[0])], axis=1)


def kernel(
    n, feat, conv_first, conv_second, query_w, key_w, value_w, output_w, time_w, gains, shifts,
    text, timestep, aug_level, text_length, out,
    x, w1, w2, wq, wk, wv, wo, wt, txt, a3, y, hid, hsend, halo1, halo2, blk, kb, vb, ones, film,
    st_send, st_recv, load_sem, st_s, st_r, halo_s, halo_r,
):
    images, band, cols, channels = feat.shape
    tokens = text.shape[1]
    cells = band * cols
    tiles = channels // LANES
    per_group = channels // GROUPS
    count = float(cells * n * per_group)
    me = lax.axis_index("rows")

    loads = [
        pltpu.make_async_copy(src, dst, load_sem.at[i])
        for i, (src, dst) in enumerate(
            [(feat.at[i], x.at[i]) for i in range(images)]
            + [(text, txt), (key_w, wk), (value_w, wv), (time_w, wt), (conv_first, w1)]
            + [(conv_second, w2), (query_w, wq), (output_w, wo)]
        )
    ]
    for load in loads:
        load.start()
    text_load, key_load, value_load, time_load, first_load, second_load, query_load, out_load = (
        loads[images:]
    )

    barrier = pltpu.get_barrier_semaphore()
    for d in range(1, n):
        pl.semaphore_signal(
            barrier, inc=1, device_id={"rows": lax.rem(me + d, n)}, device_id_type=MESH
        )

    def stat_copies(phase, first, size):
        slot = 0 if phase == 0 else 1 + first - images
        return [
            pltpu.make_async_remote_copy(
                src_ref=st_send.at[pl.ds(first, size)],
                dst_ref=st_recv.at[d, pl.ds(first, size)],
                send_sem=st_s.at[slot, d],
                recv_sem=st_r.at[slot, d],
                device_id={"rows": lax.rem(me + d, n)},
                device_id_type=MESH,
            )
            for d in range(1, n)
        ]

    def halo_copy(phase, image, way, src, halo):
        return pltpu.make_async_remote_copy(
            src_ref=src,
            dst_ref=halo.at[image, way],
            send_sem=halo_s.at[phase, image, way],
            recv_sem=halo_r.at[phase, image, way],
            device_id={"rows": me + 1 if way == 0 else me - 1},
            device_id_type=MESH,
        )

    def halo_do(phase, image, rows, halo, what):
        @pl.when(me < n - 1)
        def _():
            getattr(halo_copy(phase, image, 0, rows.at[image, band - 1], halo), what)()

        @pl.when(me > 0)
        def _():
            getattr(halo_copy(phase, image, 1, rows.at[image, 0], halo), what)()

    def norm_terms(index, image, which):
        total = st_send[index]
        for d in range(1, n):
            total = total + st_recv[d, index]
        total = group_totals(total, per_group) * (1.0 / count)
        mean, square = total[:tiles], total[tiles:]
        gain = gains[which : which + 1, :]
        scale = wide(lax.rsqrt(square - mean * mean + EPSILON)) * gain
        return scale, shifts[which : which + 1, :] - wide(mean) * scale

    def activate(read, image, scale, shift, places):
        def body(c, carry):
            start = pl.multiple_of(c * CHUNK, CHUNK)
            half = read(start).astype(F32) * scale + shift
            value = (half * jnp.tanh(half) + half).astype(BF16)
            for row, p in places:
                a3[image, pl.ds(row * cols + start, CHUNK), p * channels : (p + 1) * channels] = value
            return carry

        lax.fori_loop(0, cols // CHUNK, body, 0)

    def blank(image, row, p):
        def body(c, carry):
            start = pl.multiple_of(c * CHUNK, CHUNK)
            a3[image, pl.ds(row * cols + start, CHUNK), p * channels : (p + 1) * channels] = (
                jnp.zeros((CHUNK, channels), BF16)
            )
            return carry

        lax.fori_loop(0, cols // CHUNK, body, 0)

    def spots(row):
        return [(row - p + 1, p) for p in range(3) if 0 <= row - p + 1 < band]

    def activate_all(phase, image, read, rows, halo, scale, shift):
        scale, shift = scale * 0.5, shift * 0.5
        for row in range(band):
            activate(functools.partial(read, row), image, scale, shift, spots(row))
        for way, row, here in ((0, -1, me > 0), (1, band, me < n - 1)):
            (place,) = spots(row)

            @pl.when(here)
            def _(way=way, place=place):
                halo_copy(phase, image, way, rows.at[image, 0], halo).wait_recv()
                activate(
                    lambda start: halo[image, way, pl.ds(start, CHUNK), :],
                    image, scale, shift, [place],
                )

            @pl.when(jnp.logical_not(here))
            def _(place=place):
                blank(image, *place)

    def convolve(image, w, finish):
        for q in range(3):
            y[q] = jnp.dot(
                a3[image], w[:, q].reshape(3 * channels, channels), preferred_element_type=F32
            )
        column = lax.broadcasted_iota(jnp.int32, (cols, LANES), 0)
        sums, squares = [], []
        for tile in range(tiles):
            lanes = slice(tile * LANES, (tile + 1) * LANES)
            total, square = 0.0, 0.0
            for row in range(band):
                here = slice(row * cols, (row + 1) * cols)
                left = jnp.where(column == 0, 0.0, pltpu.roll(y[0, here, lanes], 1, axis=0))
                right = jnp.where(
                    column == cols - 1, 0.0, pltpu.roll(y[2, here, lanes], cols - 1, axis=0)
                )
                value = finish(row, here, lanes, y[1, here, lanes] + left + right)
                total = total + jnp.sum(value, axis=0, keepdims=True)
                square = square + jnp.sum(value * value, axis=0, keepdims=True)
            sums.append(total)
            squares.append(square)
        return jnp.concatenate(sums + squares, axis=0)

    for image in range(images):
        loads[image].wait()
        total = jnp.zeros((8, channels), F32)
        square = jnp.zeros((8, channels), F32)
        for row in range(band):

            def add(c, carry):
                total, square = carry
                start = pl.multiple_of(c * CHUNK, CHUNK)
                value = x[image, row, pl.ds(start, CHUNK), :].astype(F32)
                for i in range(CHUNK // 8):
                    part = value[i * 8 : (i + 1) * 8]
                    total = total + part
                    square = square + part * part
                return total, square

            total, square = lax.fori_loop(0, cols // CHUNK, add, (total, square))
        total = jnp.sum(total, axis=0, keepdims=True)
        square = jnp.sum(square, axis=0, keepdims=True)
        st_send[image] = jnp.concatenate(
            [v[:, t * LANES : (t + 1) * LANES] for v in (total, square) for t in range(tiles)],
            axis=0,
        )
    pl.semaphore_wait(barrier, n - 1)
    sent = stat_copies(0, 0, images)
    for copy in sent:
        copy.start()
    for image in range(images):
        halo_do(0, image, x, halo1, "start")

    quads = kb.shape[1]
    per_quad = HEADS // quads
    width = per_quad * HEAD_DIM
    head_of_lane = lax.broadcasted_iota(jnp.int32, (tokens, width), 1) // HEAD_DIM
    text_load.wait()
    key_load.wait()
    value_load.wait()
    for image in range(images):
        keys = jnp.dot(txt[image], wk[...], preferred_element_type=F32).astype(BF16).astype(F32)
        values = jnp.dot(txt[image], wv[...], preferred_element_type=F32)
        for quad in range(quads):
            lanes = slice(quad * width, (quad + 1) * width)
            for head in range(per_quad):
                rows = slice(head * tokens, (head + 1) * tokens)
                mine = head_of_lane == head
                kb[image, quad, rows, :] = jnp.where(
                    mine, keys[:, lanes] * HEAD_DIM**-0.5, 0.0
                ).astype(BF16)
                vb[image, quad, rows, :] = jnp.where(mine, values[:, lanes], 0.0).astype(BF16)
    for head in range(per_quad):
        ones[head * tokens : (head + 1) * tokens, :] = jnp.where(
            head_of_lane == head, 1.0, 0.0
        ).astype(BF16)
    lane = lax.broadcasted_iota(jnp.int32, (16, 4 * TFREQ), 1)
    image_of_row = lax.broadcasted_iota(jnp.int32, (16, 4 * TFREQ), 0)
    step_value = jnp.zeros((16, 4 * TFREQ), F32)
    for image in range(images):
        here = jnp.where(lane < 2 * TFREQ, timestep[image], aug_level[image]).astype(F32)
        step_value = jnp.where(image_of_row == image, here, step_value)
    angle = step_value * jnp.exp((lane % TFREQ).astype(F32) * (-math.log(10000.0) / TFREQ))
    quarter = jnp.where(lane % (2 * TFREQ) < TFREQ, 0.0, 0.5 * math.pi)
    time_load.wait()
    film[...] = jnp.dot(sine(angle + quarter).astype(BF16), wt[...], preferred_element_type=F32)

    for copy in sent:
        copy.wait_recv()
    terms = [norm_terms(image, image, 0) for image in range(images)]
    pending = list(sent)
    first_load.wait()

    for image in range(images):

        def read_x(row, start, image=image):
            return x[image, row, pl.ds(start, CHUNK), :]

        activate_all(0, image, read_x, x, halo1, *terms[image])

        def keep(row, here, lanes, value, image=image):
            hid[image, here, lanes] = value
            hsend[image, row, :, lanes] = value.astype(BF16)
            return value

        st_send[images + image] = convolve(image, w1, keep)
        sent = stat_copies(1, images + image, 1)
        for copy in sent:
            copy.start()
        pending.append(sent)
        halo_do(1, image, hsend, halo2, "start")

    second_load.wait()
    for image in range(images):
        for copy in pending[len(pending) - images]:
            copy.wait_recv()
        scale, shift = norm_terms(images + image, image, 1)
        grow = 1.0 + film[image : image + 1, :channels]
        scale, shift = scale * grow, shift * grow + film[image : image + 1, channels:]

        def read_hid(row, start, image=image):
            return hid[image, pl.ds(row * cols + start, CHUNK), :]

        activate_all(1, image, read_hid, hsend, halo2, scale, shift)

        def add_residual(row, here, lanes, value, image=image):
            rounded = (x[image, row, :, lanes].astype(F32) + value).astype(BF16)
            blk[image, here, lanes] = rounded
            return rounded.astype(F32)

        st_send[2 * images + image] = convolve(image, w2, add_residual)
        sent = stat_copies(2, 2 * images + image, 1)
        for copy in sent:
            copy.start()
        pending.append(sent)

    query_load.wait()
    out_load.wait()
    for image in range(images):
        for copy in pending[len(pending) - images + image]:
            copy.wait_recv()
        scale, shift = norm_terms(2 * images + image, image, 2)
        length = text_length[image]

        for row in range(band):
            here = slice(row * cols, (row + 1) * cols)
            block = blk[image, here, :].astype(F32)
            normed = (block * scale + shift).astype(BF16)
            queries = jnp.dot(normed, wq[...], preferred_element_type=F32).astype(BF16)
            mixed = []
            for quad in range(quads):
                scores = lax.dot_general(
                    queries[:, quad * width : (quad + 1) * width],
                    kb[image, quad],
                    (((1,), (1,)), ((), ())),
                    preferred_element_type=F32,
                )
                token = lax.broadcasted_iota(jnp.int32, (cols, tokens), 1)
                raised = []
                for head in range(per_quad):
                    score = jnp.where(
                        token < length, scores[:, head * tokens : (head + 1) * tokens], -jnp.inf
                    )
                    highest = jnp.max(score, axis=1, keepdims=True)
                    raised.append(jnp.exp(score - highest).astype(BF16))
                raised = jnp.concatenate(raised, axis=1)
                top = jnp.dot(raised, vb[image, quad], preferred_element_type=F32)
                bottom = jnp.dot(raised, ones[...], preferred_element_type=F32)
                mixed.append((top / bottom).astype(BF16))
            mixed = jnp.concatenate(mixed, axis=1)
            projected = jnp.dot(mixed, wo[...], preferred_element_type=F32)
            out[image, row] = (blk[image, here, :].astype(F32) + projected).astype(BF16)

    for item in pending:
        for copy in item if isinstance(item, list) else [item]:
            copy.wait_send()
    for image in range(images):
        halo_do(0, image, x, halo1, "wait_send")
        halo_do(1, image, hsend, halo2, "wait_send")


def shards(*args):
    features, text = args[0], args[10]
    images, band, cols, channels = features.shape
    tokens = text.shape[1]
    cells = band * cols
    n = lax.axis_size("rows")
    quads = max(1, HEADS * HEAD_DIM // 256)
    width = HEADS * HEAD_DIM // quads
    stacked = width // HEAD_DIM * tokens
    any_space = pl.BlockSpec(memory_space=pl.ANY)
    vmem = pl.BlockSpec(memory_space=pltpu.VMEM)
    smem = pl.BlockSpec(memory_space=pltpu.SMEM)
    dma = pltpu.SemaphoreType.DMA
    return pl.pallas_call(
        functools.partial(kernel, n),
        out_shape=jax.ShapeDtypeStruct(features.shape, BF16),
        in_specs=[any_space] * 8 + [vmem] * 2 + [any_space] + [smem] * 3,
        out_specs=vmem,
        scratch_shapes=[
            pltpu.VMEM(features.shape, BF16),
            pltpu.VMEM(args[1].shape, BF16),
            pltpu.VMEM(args[2].shape, BF16),
            pltpu.VMEM(args[3].shape, BF16),
            pltpu.VMEM(args[4].shape, BF16),
            pltpu.VMEM(args[5].shape, BF16),
            pltpu.VMEM(args[6].shape, BF16),
            pltpu.VMEM(args[7].shape, BF16),
            pltpu.VMEM(text.shape, BF16),
            pltpu.VMEM((images, cells, 3 * channels), BF16),
            pltpu.VMEM((3, cells, channels), F32),
            pltpu.VMEM((images, cells, channels), F32),
            pltpu.VMEM(features.shape, BF16),
            pltpu.VMEM((images, 2, cols, channels), BF16),
            pltpu.VMEM((images, 2, cols, channels), BF16),
            pltpu.VMEM((images, cells, channels), BF16),
            pltpu.VMEM((images, quads, stacked, width), BF16),
            pltpu.VMEM((images, quads, stacked, width), BF16),
            pltpu.VMEM((stacked, width), BF16),
            pltpu.VMEM((16, 2 * channels), F32),
            pltpu.VMEM((3 * images, 2 * channels // LANES, LANES), F32),
            pltpu.VMEM((n, 3 * images, 2 * channels // LANES, LANES), F32),
            dma((images + 8,)),
            dma((1 + 2 * images, n)),
            dma((1 + 2 * images, n)),
            dma((2, images, 2)),
            dma((2, images, 2)),
        ],
        compiler_params=pltpu.CompilerParams(
            collective_id=0, has_side_effects=True, vmem_limit_bytes=56 * 1024 * 1024
        ),
    )(*args)


def solution(mesh):
    placed = (
        P("img", "rows", None, None),
        P(),
        P(),
        P(),
        P(),
        P(),
        P(),
        P(),
        P(),
        P(),
        P("img", None, None),
        P("img"),
        P("img"),
        P("img"),
    )
    return jax.shard_map(
        shards, mesh=mesh, in_specs=placed, out_specs=P("img", "rows", None, None), check_vma=False
    )
```

```python
import functools
import math

import jax
import jax.numpy as jnp
from jax import lax
from jax.experimental import pallas as pl
from jax.experimental.pallas import tpu as pltpu
from jax.sharding import PartitionSpec as P

GROUPS = 32
HEADS = 8
HEAD_DIM = 64
TFREQ = 64
EPSILON = 1e-05
LANES = 128
CHUNK = 64
STRETCH = 32
F32 = jnp.float32
BF16 = jnp.bfloat16
MESH = pl.DeviceIdType.MESH


def sine(angle):
    turns = jnp.floor(angle * (0.5 / math.pi) + 0.5)
    x = (angle - turns * 6.28125) - turns * (2.0 * math.pi - 6.28125)
    square = x * x
    total = jnp.full_like(x, 1.0 / math.factorial(17))
    for power in (15, 13, 11, 9, 7, 5, 3, 1):
        sign = -1.0 if (power // 2) % 2 else 1.0
        total = total * square + sign / math.factorial(power)
    return total * x


def group_totals(tile, size):
    lane = lax.broadcasted_iota(jnp.int32, tile.shape, 1)
    step = 1
    while step < size:
        up = pltpu.roll(tile, LANES - step, axis=1)
        down = pltpu.roll(tile, step, axis=1)
        tile = tile + jnp.where(lane % (2 * step) < step, up, down)
        step *= 2
    return tile


def wide(tile):
    return jnp.concatenate([tile[i : i + 1] for i in range(tile.shape[0])], axis=1)


def kernel(
    n, x, conv_first, conv_second, wq, wk, wv, wo, wt, gains, shifts,
    txt, timestep, aug_level, text_length, out,
    w1, w2, a3, hid, hsend, halo1, halo2, blk, kb, vb, ones, film, affine,
    st_send, st_recv, load_sem, st_s, st_r, halo_s, halo_r,
):
    images, band, cols, channels = x.shape
    tokens = txt.shape[1]
    cells = band * cols
    tiles = channels // LANES
    per_group = channels // GROUPS
    count = float(cells * n * per_group)
    me = lax.axis_index("rows")

    first_load = pltpu.make_async_copy(conv_first, w1, load_sem.at[0])
    second_load = pltpu.make_async_copy(conv_second, w2, load_sem.at[1])
    first_load.start()
    second_load.start()

    barrier = pltpu.get_barrier_semaphore()
    for d in range(1, n):
        pl.semaphore_signal(
            barrier, inc=1, device_id={"rows": lax.rem(me + d, n)}, device_id_type=MESH
        )

    def stat_copies(phase, first, size):
        slot = 0 if phase == 0 else 1 + first - images
        return [
            pltpu.make_async_remote_copy(
                src_ref=st_send.at[pl.ds(first, size)],
                dst_ref=st_recv.at[d, pl.ds(first, size)],
                send_sem=st_s.at[slot, d],
                recv_sem=st_r.at[slot, d],
                device_id={"rows": lax.rem(me + d, n)},
                device_id_type=MESH,
            )
            for d in range(1, n)
        ]

    def halo_copy(phase, image, way, src, halo):
        return pltpu.make_async_remote_copy(
            src_ref=src,
            dst_ref=halo.at[image, way],
            send_sem=halo_s.at[phase, image, way],
            recv_sem=halo_r.at[phase, image, way],
            device_id={"rows": me + 1 if way == 0 else me - 1},
            device_id_type=MESH,
        )

    def halo_do(phase, image, rows, halo, what):
        @pl.when(me < n - 1)
        def _():
            getattr(halo_copy(phase, image, 0, rows.at[image, band - 1], halo), what)()

        @pl.when(me > 0)
        def _():
            getattr(halo_copy(phase, image, 1, rows.at[image, 0], halo), what)()

    def norm_terms(index, image, which):
        total = st_send[index]
        for d in range(1, n):
            total = total + st_recv[d, index]
        total = group_totals(total, per_group) * (1.0 / count)
        mean, square = total[:tiles], total[tiles:]
        gain = gains[which : which + 1, :]
        scale = wide(lax.rsqrt(square - mean * mean + EPSILON)) * gain
        return scale, shifts[which : which + 1, :] - wide(mean) * scale

    def place_at(row, p, q, lane):
        start = pl.multiple_of((p * 3 + q) * channels + lane, LANES)
        return slice(row * cols, (row + 1) * cols), pl.ds(start, LANES)

    def activate(read, image, places):
        def body(tile, carry):
            lane = pl.multiple_of(tile * LANES, LANES)
            column = lax.broadcasted_iota(jnp.int32, (cols, LANES), 0)
            half = read(lane).astype(F32) * affine[0:1, pl.ds(lane, LANES)]
            half = half + affine[1:2, pl.ds(lane, LANES)]
            value = half * jnp.tanh(half) + half
            left = jnp.where(column == 0, 0.0, pltpu.roll(value, 1, axis=0))
            right = jnp.where(column == cols - 1, 0.0, pltpu.roll(value, cols - 1, axis=0))
            for q, tap in enumerate((left, value, right)):
                tap = tap.astype(BF16)
                for row, p in places:
                    rows, lanes = place_at(row, p, q, lane)
                    a3[image, rows, lanes] = tap
            return carry

        lax.fori_loop(0, tiles, body, 0)

    def blank(image, row, p):
        a3[image, row * cols : (row + 1) * cols, 3 * p * channels : 3 * (p + 1) * channels] = (
            jnp.zeros((cols, 3 * channels), BF16)
        )

    def spots(row):
        return [(row - p + 1, p) for p in range(3) if 0 <= row - p + 1 < band]

    def activate_all(phase, image, read, rows, halo, scale, shift):
        affine[0:1, :] = scale * 0.5
        affine[1:2, :] = shift * 0.5
        for row in range(band):
            activate(functools.partial(read, row), image, spots(row))
        for way, row, here in ((0, -1, me > 0), (1, band, me < n - 1)):
            (place,) = spots(row)

            @pl.when(here)
            def _(way=way, place=place):
                halo_copy(phase, image, way, rows.at[image, 0], halo).wait_recv()
                activate(lambda lane: halo[image, way, :, pl.ds(lane, LANES)], image, [place])

            @pl.when(jnp.logical_not(here))
            def _(place=place):
                blank(image, *place)

    def convolve(image, w, finish):
        hid[image] = jnp.dot(
            a3[image], w[...].reshape(9 * channels, channels), preferred_element_type=F32
        )
        total = jnp.zeros((8, channels), F32)
        square = jnp.zeros((8, channels), F32)
        for row in range(band):

            def add(c, carry, row=row):
                total, square = carry
                start = pl.multiple_of(c * STRETCH, STRETCH)
                here = pl.ds(row * cols + start, STRETCH)
                value = finish(row, pl.ds(start, STRETCH), here, hid[image, here, :])
                for i in range(STRETCH // 8):
                    part = value[i * 8 : (i + 1) * 8]
                    total = total + part
                    square = square + part * part
                return total, square

            total, square = lax.fori_loop(0, cols // STRETCH, add, (total, square))
        return stat_tile(total, square)

    def stat_tile(total, square):
        total = jnp.sum(total, axis=0, keepdims=True)
        square = jnp.sum(square, axis=0, keepdims=True)
        return jnp.concatenate(
            [v[:, t * LANES : (t + 1) * LANES] for v in (total, square) for t in range(tiles)],
            axis=0,
        )

    for image in range(images):
        total = jnp.zeros((8, channels), F32)
        square = jnp.zeros((8, channels), F32)
        for row in range(band):

            def add(c, carry):
                total, square = carry
                start = pl.multiple_of(c * CHUNK, CHUNK)
                value = x[image, row, pl.ds(start, CHUNK), :].astype(F32)
                for i in range(CHUNK // 8):
                    part = value[i * 8 : (i + 1) * 8]
                    total = total + part
                    square = square + part * part
                return total, square

            total, square = lax.fori_loop(0, cols // CHUNK, add, (total, square))
        st_send[image] = stat_tile(total, square)
    pl.semaphore_wait(barrier, n - 1)
    sent = stat_copies(0, 0, images)
    for copy in sent:
        copy.start()
    for image in range(images):
        halo_do(0, image, x, halo1, "start")

    quads = kb.shape[1]
    per_quad = HEADS // quads
    width = per_quad * HEAD_DIM
    head_of_lane = lax.broadcasted_iota(jnp.int32, (tokens, width), 1) // HEAD_DIM
    for image in range(images):
        keys = jnp.dot(txt[image], wk[...], preferred_element_type=F32).astype(BF16).astype(F32)
        values = jnp.dot(txt[image], wv[...], preferred_element_type=F32)
        for quad in range(quads):
            lanes = slice(quad * width, (quad + 1) * width)
            for head in range(per_quad):
                rows = slice(head * tokens, (head + 1) * tokens)
                mine = head_of_lane == head
                kb[image, quad, rows, :] = jnp.where(
                    mine, keys[:, lanes] * HEAD_DIM**-0.5, 0.0
                ).astype(BF16)
                vb[image, quad, rows, :] = jnp.where(mine, values[:, lanes], 0.0).astype(BF16)
    for head in range(per_quad):
        ones[head * tokens : (head + 1) * tokens, :] = jnp.where(
            head_of_lane == head, 1.0, 0.0
        ).astype(BF16)
    lane = lax.broadcasted_iota(jnp.int32, (16, 4 * TFREQ), 1)
    image_of_row = lax.broadcasted_iota(jnp.int32, (16, 4 * TFREQ), 0)
    step_value = jnp.zeros((16, 4 * TFREQ), F32)
    for image in range(images):
        here = jnp.where(lane < 2 * TFREQ, timestep[image], aug_level[image]).astype(F32)
        step_value = jnp.where(image_of_row == image, here, step_value)
    angle = step_value * jnp.exp((lane % TFREQ).astype(F32) * (-math.log(10000.0) / TFREQ))
    quarter = jnp.where(lane % (2 * TFREQ) < TFREQ, 0.0, 0.5 * math.pi)
    film[...] = jnp.dot(sine(angle + quarter).astype(BF16), wt[...], preferred_element_type=F32)

    for copy in sent:
        copy.wait_recv()
    terms = [norm_terms(image, image, 0) for image in range(images)]
    pending = list(sent)
    first_load.wait()

    for image in range(images):

        def read_x(row, lane, image=image):
            return x[image, row, :, pl.ds(lane, LANES)]

        activate_all(0, image, read_x, x, halo1, *terms[image])

        def keep(row, columns, here, value, image=image):
            hsend[image, row, columns, :] = value.astype(BF16)
            return value

        st_send[images + image] = convolve(image, w1, keep)
        sent = stat_copies(1, images + image, 1)
        for copy in sent:
            copy.start()
        pending.append(sent)
        halo_do(1, image, hsend, halo2, "start")

    second_load.wait()
    for image in range(images):
        for copy in pending[len(pending) - images]:
            copy.wait_recv()
        scale, shift = norm_terms(images + image, image, 1)
        grow = 1.0 + film[image : image + 1, :channels]
        scale, shift = scale * grow, shift * grow + film[image : image + 1, channels:]

        def read_hid(row, lane, image=image):
            return hid[image, row * cols : (row + 1) * cols, pl.ds(lane, LANES)]

        activate_all(1, image, read_hid, hsend, halo2, scale, shift)

        def add_residual(row, columns, here, value, image=image):
            rounded = (x[image, row, columns, :].astype(F32) + value).astype(BF16)
            blk[image, here, :] = rounded
            return rounded.astype(F32)

        st_send[2 * images + image] = convolve(image, w2, add_residual)
        sent = stat_copies(2, 2 * images + image, 1)
        for copy in sent:
            copy.start()
        pending.append(sent)

    for image in range(images):
        for copy in pending[len(pending) - images + image]:
            copy.wait_recv()
        scale, shift = norm_terms(2 * images + image, image, 2)
        length = text_length[image]

        for row in range(band):
            here = slice(row * cols, (row + 1) * cols)
            block = blk[image, here, :].astype(F32)
            normed = (block * scale + shift).astype(BF16)
            queries = jnp.dot(normed, wq[...], preferred_element_type=F32).astype(BF16)
            mixed = []
            for quad in range(quads):
                scores = lax.dot_general(
                    queries[:, quad * width : (quad + 1) * width],
                    kb[image, quad],
                    (((1,), (1,)), ((), ())),
                    preferred_element_type=F32,
                )
                token = lax.broadcasted_iota(jnp.int32, (cols, tokens), 1)
                raised = []
                for head in range(per_quad):
                    score = jnp.where(
                        token < length, scores[:, head * tokens : (head + 1) * tokens], -jnp.inf
                    )
                    highest = jnp.max(score, axis=1, keepdims=True)
                    raised.append(jnp.exp(score - highest).astype(BF16))
                raised = jnp.concatenate(raised, axis=1)
                top = jnp.dot(raised, vb[image, quad], preferred_element_type=F32)
                bottom = jnp.dot(raised, ones[...], preferred_element_type=F32)
                mixed.append((top / bottom).astype(BF16))
            mixed = jnp.concatenate(mixed, axis=1)
            projected = jnp.dot(mixed, wo[...], preferred_element_type=F32)
            out[image, row] = (blk[image, here, :].astype(F32) + projected).astype(BF16)

    for item in pending:
        for copy in item if isinstance(item, list) else [item]:
            copy.wait_send()
    for image in range(images):
        halo_do(0, image, x, halo1, "wait_send")
        halo_do(1, image, hsend, halo2, "wait_send")


def shards(*args):
    features, text = args[0], args[10]
    images, band, cols, channels = features.shape
    tokens = text.shape[1]
    cells = band * cols
    n = lax.axis_size("rows")
    quads = max(1, HEADS * HEAD_DIM // 256)
    width = HEADS * HEAD_DIM // quads
    stacked = width // HEAD_DIM * tokens
    any_space = pl.BlockSpec(memory_space=pl.ANY)
    vmem = pl.BlockSpec(memory_space=pltpu.VMEM)
    smem = pl.BlockSpec(memory_space=pltpu.SMEM)
    dma = pltpu.SemaphoreType.DMA
    return pl.pallas_call(
        functools.partial(kernel, n),
        out_shape=jax.ShapeDtypeStruct(features.shape, BF16),
        in_specs=[vmem] + [any_space] * 2 + [vmem] * 8 + [smem] * 3,
        out_specs=vmem,
        scratch_shapes=[
            pltpu.VMEM(args[1].shape, BF16),
            pltpu.VMEM(args[2].shape, BF16),
            pltpu.VMEM((images, cells, 9 * channels), BF16),
            pltpu.VMEM((images, cells, channels), F32),
            pltpu.VMEM(features.shape, BF16),
            pltpu.VMEM((images, 2, cols, channels), BF16),
            pltpu.VMEM((images, 2, cols, channels), BF16),
            pltpu.VMEM((images, cells, channels), BF16),
            pltpu.VMEM((images, quads, stacked, width), BF16),
            pltpu.VMEM((images, quads, stacked, width), BF16),
            pltpu.VMEM((stacked, width), BF16),
            pltpu.VMEM((16, 2 * channels), F32),
            pltpu.VMEM((8, channels), F32),
            pltpu.VMEM((3 * images, 2 * channels // LANES, LANES), F32),
            pltpu.VMEM((n, 3 * images, 2 * channels // LANES, LANES), F32),
            dma((2,)),
            dma((1 + 2 * images, n)),
            dma((1 + 2 * images, n)),
            dma((2, images, 2)),
            dma((2, images, 2)),
        ],
        compiler_params=pltpu.CompilerParams(
            collective_id=0, has_side_effects=True, vmem_limit_bytes=48 * 1024 * 1024
        ),
    )(*args)


def solution(mesh):
    placed = (
        P("img", "rows", None, None),
        P(),
        P(),
        P(),
        P(),
        P(),
        P(),
        P(),
        P(),
        P(),
        P("img", None, None),
        P("img"),
        P("img"),
        P("img"),
    )
    return jax.shard_map(
        shards, mesh=mesh, in_specs=placed, out_specs=P("img", "rows", None, None), check_vma=False
    )
```

```python
import functools
import math

import jax
import jax.numpy as jnp
from jax import lax
from jax.experimental import pallas as pl
from jax.experimental.pallas import tpu as pltpu
from jax.sharding import PartitionSpec as P

GROUPS = 32
HEADS = 8
HEAD_DIM = 64
TFREQ = 64
EPSILON = 1e-05
LANES = 128
CHUNK = 64
F32 = jnp.float32
BF16 = jnp.bfloat16
MESH = pl.DeviceIdType.MESH


def sine(angle):
    turns = jnp.floor(angle * (0.5 / math.pi) + 0.5)
    x = (angle - turns * 6.28125) - turns * (2.0 * math.pi - 6.28125)
    square = x * x
    total = jnp.full_like(x, 1.0 / math.factorial(17))
    for power in (15, 13, 11, 9, 7, 5, 3, 1):
        sign = -1.0 if (power // 2) % 2 else 1.0
        total = total * square + sign / math.factorial(power)
    return total * x


def group_totals(tile, size):
    lane = lax.broadcasted_iota(jnp.int32, tile.shape, 1)
    step = 1
    while step < size:
        up = pltpu.roll(tile, LANES - step, axis=1)
        down = pltpu.roll(tile, step, axis=1)
        tile = tile + jnp.where(lane % (2 * step) < step, up, down)
        step *= 2
    return tile


def pack(tile, tiles, size):
    tile = group_totals(tile, size)
    lane = lax.broadcasted_iota(jnp.int32, tile.shape, 1)
    row = lax.broadcasted_iota(jnp.int32, tile.shape, 0)
    mine = jnp.where(lane % tiles == row % tiles, tile, 0.0)
    return jnp.concatenate(
        [jnp.sum(mine[i * tiles : (i + 1) * tiles], axis=0, keepdims=True) for i in range(2)], axis=0
    )


def unpack(packed, tiles):
    tile = jnp.concatenate(
        [jnp.broadcast_to(packed[i : i + 1], (tiles, LANES)) for i in range(2)], axis=0
    )
    lane = lax.broadcasted_iota(jnp.int32, tile.shape, 1)
    row = lax.broadcasted_iota(jnp.int32, tile.shape, 0)
    return group_totals(jnp.where(lane % tiles == row % tiles, tile, 0.0), tiles)


def wide(tile):
    return jnp.concatenate([tile[i : i + 1] for i in range(tile.shape[0])], axis=1)


def kernel(
    n, feat, conv_first, conv_second, query_w, key_w, value_w, output_w, time_w, gains, shifts,
    text, timestep, aug_level, text_length, out,
    x, w1, w2, wq, wk, wv, wo, wt, txt, a3, y, hid, hsend, halo1, halo2, blk, kb, vb, ones, film,
    st_send, st_recv, load_sem, st_s, st_r, halo_s, halo_r,
):
    images, band, cols, channels = feat.shape
    tokens = text.shape[1]
    cells = band * cols
    tiles = channels // LANES
    per_group = channels // GROUPS
    count = float(cells * n * per_group)
    me = lax.axis_index("rows")

    loads = [
        pltpu.make_async_copy(src, dst, load_sem.at[i])
        for i, (src, dst) in enumerate(
            [(feat.at[i], x.at[i]) for i in range(images)]
            + [(text, txt), (key_w, wk), (value_w, wv), (time_w, wt), (conv_first, w1)]
            + [(conv_second, w2), (query_w, wq), (output_w, wo)]
        )
    ]
    for load in loads:
        load.start()
    text_load, key_load, value_load, time_load, first_load, second_load, query_load, out_load = (
        loads[images:]
    )

    barrier = pltpu.get_barrier_semaphore()
    for d in range(1, n):
        pl.semaphore_signal(
            barrier, inc=1, device_id={"rows": lax.rem(me + d, n)}, device_id_type=MESH
        )

    def stat_copies(phase, first, size):
        slot = 0 if phase == 0 else 1 + first - images
        return [
            pltpu.make_async_remote_copy(
                src_ref=st_send.at[pl.ds(first, size)],
                dst_ref=st_recv.at[d, pl.ds(first, size)],
                send_sem=st_s.at[slot, d],
                recv_sem=st_r.at[slot, d],
                device_id={"rows": lax.rem(me + d, n)},
                device_id_type=MESH,
            )
            for d in range(1, n)
        ]

    def halo_copy(phase, image, way, src, halo):
        return pltpu.make_async_remote_copy(
            src_ref=src,
            dst_ref=halo.at[image, way],
            send_sem=halo_s.at[phase, image, way],
            recv_sem=halo_r.at[phase, image, way],
            device_id={"rows": me + 1 if way == 0 else me - 1},
            device_id_type=MESH,
        )

    def halo_do(phase, image, rows, halo, what):
        @pl.when(me < n - 1)
        def _():
            getattr(halo_copy(phase, image, 0, rows.at[image, band - 1], halo), what)()

        @pl.when(me > 0)
        def _():
            getattr(halo_copy(phase, image, 1, rows.at[image, 0], halo), what)()

    def norm_terms(index, image, which):
        total = st_send[index]
        for d in range(1, n):
            total = total + st_recv[d, index]
        total = unpack(total, tiles) * (1.0 / count)
        mean, square = total[:tiles], total[tiles:]
        gain = gains[which : which + 1, :]
        scale = wide(lax.rsqrt(square - mean * mean + EPSILON)) * gain
        return scale, shifts[which : which + 1, :] - wide(mean) * scale

    def activate(read, image, scale, shift, places):
        def body(c, carry):
            start = pl.multiple_of(c * CHUNK, CHUNK)
            half = read(start).astype(F32) * scale + shift
            value = (half * jnp.tanh(half) + half).astype(BF16)
            for row, p in places:
                a3[image, pl.ds(row * cols + start, CHUNK), p * channels : (p + 1) * channels] = value
            return carry

        lax.fori_loop(0, cols // CHUNK, body, 0)

    def blank(image, row, p):
        def body(c, carry):
            start = pl.multiple_of(c * CHUNK, CHUNK)
            a3[image, pl.ds(row * cols + start, CHUNK), p * channels : (p + 1) * channels] = (
                jnp.zeros((CHUNK, channels), BF16)
            )
            return carry

        lax.fori_loop(0, cols // CHUNK, body, 0)

    def spots(row):
        return [(row - p + 1, p) for p in range(3) if 0 <= row - p + 1 < band]

    def activate_own(image, read, scale, shift):
        for row in range(band):
            activate(functools.partial(read, row), image, scale * 0.5, shift * 0.5, spots(row))

    def activate_halo(phase, image, rows, halo, scale, shift):
        for way, row, here in ((0, -1, me > 0), (1, band, me < n - 1)):
            (place,) = spots(row)

            @pl.when(here)
            def _(way=way, place=place):
                halo_copy(phase, image, way, rows.at[image, 0], halo).wait_recv()
                activate(
                    lambda start: halo[image, way, pl.ds(start, CHUNK), :],
                    image, scale * 0.5, shift * 0.5, [place],
                )

            @pl.when(jnp.logical_not(here))
            def _(place=place):
                blank(image, *place)

    def convolve(image, w, finish):
        for q in range(3):
            y[q] = jnp.dot(
                a3[image], w[:, q].reshape(3 * channels, channels), preferred_element_type=F32
            )
        column = lax.broadcasted_iota(jnp.int32, (cols, LANES), 0)
        sums, squares = [], []
        for tile in range(tiles):
            lanes = slice(tile * LANES, (tile + 1) * LANES)
            total, square = 0.0, 0.0
            for row in range(band):
                here = slice(row * cols, (row + 1) * cols)
                left = jnp.where(column == 0, 0.0, pltpu.roll(y[0, here, lanes], 1, axis=0))
                right = jnp.where(
                    column == cols - 1, 0.0, pltpu.roll(y[2, here, lanes], cols - 1, axis=0)
                )
                value = finish(row, here, lanes, y[1, here, lanes] + left + right)
                total = total + jnp.sum(value, axis=0, keepdims=True)
                square = square + jnp.sum(value * value, axis=0, keepdims=True)
            sums.append(total)
            squares.append(square)
        return pack(jnp.concatenate(sums + squares, axis=0), tiles, per_group)

    for image in range(images):
        loads[image].wait()
        total = jnp.zeros((8, channels), F32)
        square = jnp.zeros((8, channels), F32)
        for row in range(band):

            def add(c, carry):
                total, square = carry
                start = pl.multiple_of(c * CHUNK, CHUNK)
                value = x[image, row, pl.ds(start, CHUNK), :].astype(F32)
                for i in range(CHUNK // 8):
                    part = value[i * 8 : (i + 1) * 8]
                    total = total + part
                    square = square + part * part
                return total, square

            total, square = lax.fori_loop(0, cols // CHUNK, add, (total, square))
        total = jnp.sum(total, axis=0, keepdims=True)
        square = jnp.sum(square, axis=0, keepdims=True)
        packed = jnp.concatenate(
            [v[:, t * LANES : (t + 1) * LANES] for v in (total, square) for t in range(tiles)],
            axis=0,
        )
        st_send[image] = pack(packed, tiles, per_group)
    pl.semaphore_wait(barrier, n - 1)
    sent = stat_copies(0, 0, images)
    for copy in sent:
        copy.start()
    for image in range(images):
        halo_do(0, image, x, halo1, "start")

    quads = kb.shape[1]
    per_quad = HEADS // quads
    width = per_quad * HEAD_DIM
    head_of_lane = lax.broadcasted_iota(jnp.int32, (tokens, width), 1) // HEAD_DIM
    text_load.wait()
    key_load.wait()
    value_load.wait()
    for image in range(images):
        keys = jnp.dot(txt[image], wk[...], preferred_element_type=F32).astype(BF16).astype(F32)
        values = jnp.dot(txt[image], wv[...], preferred_element_type=F32)
        for quad in range(quads):
            lanes = slice(quad * width, (quad + 1) * width)
            for head in range(per_quad):
                rows = slice(head * tokens, (head + 1) * tokens)
                mine = head_of_lane == head
                kb[image, quad, rows, :] = jnp.where(
                    mine, keys[:, lanes] * HEAD_DIM**-0.5, 0.0
                ).astype(BF16)
                vb[image, quad, rows, :] = jnp.where(mine, values[:, lanes], 0.0).astype(BF16)
    for head in range(per_quad):
        ones[head * tokens : (head + 1) * tokens, :] = jnp.where(
            head_of_lane == head, 1.0, 0.0
        ).astype(BF16)
    lane = lax.broadcasted_iota(jnp.int32, (16, 4 * TFREQ), 1)
    image_of_row = lax.broadcasted_iota(jnp.int32, (16, 4 * TFREQ), 0)
    step_value = jnp.zeros((16, 4 * TFREQ), F32)
    for image in range(images):
        here = jnp.where(lane < 2 * TFREQ, timestep[image], aug_level[image]).astype(F32)
        step_value = jnp.where(image_of_row == image, here, step_value)
    angle = step_value * jnp.exp((lane % TFREQ).astype(F32) * (-math.log(10000.0) / TFREQ))
    quarter = jnp.where(lane % (2 * TFREQ) < TFREQ, 0.0, 0.5 * math.pi)
    time_load.wait()
    film[...] = jnp.dot(sine(angle + quarter).astype(BF16), wt[...], preferred_element_type=F32)

    for copy in sent:
        copy.wait_recv()
    terms = [norm_terms(image, image, 0) for image in range(images)]
    pending = list(sent)

    for image in range(images):

        def read_x(row, start, image=image):
            return x[image, row, pl.ds(start, CHUNK), :]

        activate_own(image, read_x, *terms[image])

    first_load.wait()
    for image in range(images):
        activate_halo(0, image, x, halo1, *terms[image])

        def keep(row, here, lanes, value, image=image):
            hid[image, here, lanes] = value
            hsend[image, row, :, lanes] = value.astype(BF16)
            return value

        st_send[images + image] = convolve(image, w1, keep)
        sent = stat_copies(1, images + image, 1)
        for copy in sent:
            copy.start()
        pending.append(sent)
        halo_do(1, image, hsend, halo2, "start")

    second_load.wait()
    for image in range(images):
        for copy in pending[len(pending) - images]:
            copy.wait_recv()
        scale, shift = norm_terms(images + image, image, 1)
        grow = 1.0 + film[image : image + 1, :channels]
        scale, shift = scale * grow, shift * grow + film[image : image + 1, channels:]

        def read_hid(row, start, image=image):
            return hid[image, pl.ds(row * cols + start, CHUNK), :]

        activate_own(image, read_hid, scale, shift)
        activate_halo(1, image, hsend, halo2, scale, shift)

        def add_residual(row, here, lanes, value, image=image):
            rounded = (x[image, row, :, lanes].astype(F32) + value).astype(BF16)
            blk[image, here, lanes] = rounded
            return rounded.astype(F32)

        st_send[2 * images + image] = convolve(image, w2, add_residual)
        sent = stat_copies(2, 2 * images + image, 1)
        for copy in sent:
            copy.start()
        pending.append(sent)

    query_load.wait()
    out_load.wait()
    for image in range(images):
        for copy in pending[len(pending) - images + image]:
            copy.wait_recv()
        scale, shift = norm_terms(2 * images + image, image, 2)
        length = text_length[image]

        for row in range(band):
            here = slice(row * cols, (row + 1) * cols)
            block = blk[image, here, :].astype(F32)
            normed = (block * scale + shift).astype(BF16)
            queries = jnp.dot(normed, wq[...], preferred_element_type=F32).astype(BF16)
            mixed = []
            for quad in range(quads):
                scores = lax.dot_general(
                    queries[:, quad * width : (quad + 1) * width],
                    kb[image, quad],
                    (((1,), (1,)), ((), ())),
                    preferred_element_type=F32,
                )
                token = lax.broadcasted_iota(jnp.int32, (cols, tokens), 1)
                raised = []
                for head in range(per_quad):
                    score = jnp.where(
                        token < length, scores[:, head * tokens : (head + 1) * tokens], -jnp.inf
                    )
                    highest = jnp.max(score, axis=1, keepdims=True)
                    raised.append(jnp.exp(score - highest).astype(BF16))
                raised = jnp.concatenate(raised, axis=1)
                top = jnp.dot(raised, vb[image, quad], preferred_element_type=F32)
                bottom = jnp.dot(raised, ones[...], preferred_element_type=F32)
                mixed.append((top / bottom).astype(BF16))
            mixed = jnp.concatenate(mixed, axis=1)
            projected = jnp.dot(mixed, wo[...], preferred_element_type=F32)
            out[image, row] = (blk[image, here, :].astype(F32) + projected).astype(BF16)

    for item in pending:
        for copy in item if isinstance(item, list) else [item]:
            copy.wait_send()
    for image in range(images):
        halo_do(0, image, x, halo1, "wait_send")
        halo_do(1, image, hsend, halo2, "wait_send")


def shards(*args):
    features, text = args[0], args[10]
    images, band, cols, channels = features.shape
    tokens = text.shape[1]
    cells = band * cols
    n = lax.axis_size("rows")
    quads = max(1, HEADS * HEAD_DIM // 256)
    width = HEADS * HEAD_DIM // quads
    stacked = width // HEAD_DIM * tokens
    any_space = pl.BlockSpec(memory_space=pl.ANY)
    vmem = pl.BlockSpec(memory_space=pltpu.VMEM)
    smem = pl.BlockSpec(memory_space=pltpu.SMEM)
    dma = pltpu.SemaphoreType.DMA
    return pl.pallas_call(
        functools.partial(kernel, n),
        out_shape=jax.ShapeDtypeStruct(features.shape, BF16),
        in_specs=[any_space] * 8 + [vmem] * 2 + [any_space] + [smem] * 3,
        out_specs=vmem,
        scratch_shapes=[
            pltpu.VMEM(features.shape, BF16),
            pltpu.VMEM(args[1].shape, BF16),
            pltpu.VMEM(args[2].shape, BF16),
            pltpu.VMEM(args[3].shape, BF16),
            pltpu.VMEM(args[4].shape, BF16),
            pltpu.VMEM(args[5].shape, BF16),
            pltpu.VMEM(args[6].shape, BF16),
            pltpu.VMEM(args[7].shape, BF16),
            pltpu.VMEM(text.shape, BF16),
            pltpu.VMEM((images, cells, 3 * channels), BF16),
            pltpu.VMEM((3, cells, channels), F32),
            pltpu.VMEM((images, cells, channels), F32),
            pltpu.VMEM(features.shape, BF16),
            pltpu.VMEM((images, 2, cols, channels), BF16),
            pltpu.VMEM((images, 2, cols, channels), BF16),
            pltpu.VMEM((images, cells, channels), BF16),
            pltpu.VMEM((images, quads, stacked, width), BF16),
            pltpu.VMEM((images, quads, stacked, width), BF16),
            pltpu.VMEM((stacked, width), BF16),
            pltpu.VMEM((16, 2 * channels), F32),
            pltpu.VMEM((3 * images, 2, LANES), F32),
            pltpu.VMEM((n, 3 * images, 2, LANES), F32),
            dma((images + 8,)),
            dma((1 + 2 * images, n)),
            dma((1 + 2 * images, n)),
            dma((2, images, 2)),
            dma((2, images, 2)),
        ],
        compiler_params=pltpu.CompilerParams(
            collective_id=0, has_side_effects=True, vmem_limit_bytes=56 * 1024 * 1024
        ),
    )(*args)


def solution(mesh):
    placed = (
        P("img", "rows", None, None),
        P(),
        P(),
        P(),
        P(),
        P(),
        P(),
        P(),
        P(),
        P(),
        P("img", None, None),
        P("img"),
        P("img"),
        P("img"),
    )
    return jax.shard_map(
        shards, mesh=mesh, in_specs=placed, out_specs=P("img", "rows", None, None), check_vma=False
    )
```
